32 devices in a mesh: groups: 2 (over y), wide: 4 (over x, core), narrow: 4 (over z).
Axes of the slice: x: 2, y: 2, z: 4, core: 2. Of those that a mesh axis runs over, the one named last changes fastest.
Arguments:
- basis: bfloat16 [128, 64, 2, 512], P(('groups', 'wide'), 'narrow'), parts along dimension 0, may hold values from -0.25 to 0.25
- kappa: float32 [128, 64, 2], P(('groups', 'wide'), 'narrow'), parts along dimension 0, may hold values from 0.1 to 1
- velocity: float32 [3, 512], P(None, 'groups'), parts along dimension 1, may hold values from -2 to 2
- coefficients: float32 [512, 512], P('groups'), parts along dimension 0, may hold values from -6 to 6
- propagator: float32 [1024, 512], P('groups'), parts along dimension 0, may hold values from -0.25 to 0.25
Outputs:
- advanced: float32 [512, 512], P(('groups', 'wide', 'narrow')), parts along dimension 0
The draws below stay inside these ranges and needn't reach their ends.
There are 2 independent parts, one for each index of `groups`. The reference program is written for one: setup_inputs(seed, part) draws one part's arguments, and reference() takes and returns one part's arrays. A program takes and returns all parts, laid end to end along the dimension named above; each array names one. Nothing has to cross between parts.
All inputs are finite; a program needn't handle non-finite values.
Results may differ from the reference program's by a relative error of at most 0.0056.
Values may be sent and summed in bfloat16 or wider, within the bound.
A program may use at most 64 MiB of HBM per device.

```python
import math
import jax
import jax.numpy as jnp
from jax import lax

R = 512
P_SIZE = 256
CX = 16
ITERS = 2
NX = 64
NY = 64
NZ = 2
N_WIDE = 4


def block_scale(rng, dims, cuts, smallest, top_value):
    factor_of, own = 1.0, jax.random.fold_in(rng, 6)
    for position, shards_of in cuts:
        draws = jnp.exp(jax.random.uniform(jax.random.fold_in(own, position), (shards_of,), jnp.float32, smallest / len(cuts), top_value / len(cuts)))
        factor_of = factor_of * jnp.repeat(draws, dims[position] // shards_of).reshape([-1 if axis == position else 1 for axis in range(len(dims))])
    return factor_of


def noise(rng, extent, deviation, bound, cuts=(), kind=jnp.bfloat16):
    values = jax.random.normal(rng, extent, jnp.float32) * deviation
    if len(cuts) > 0:
        values = block_scale(rng, extent, cuts, -0.22, 0.18) * values
    return jnp.clip(values, min=-bound, max=bound).astype(kind)


def setup_inputs(seed: int = 0, part: int = 0) -> dict:
    keys = jax.random.split(jax.random.key(seed), 6)
    part_splits = jax.random.split(jax.random.fold_in(keys[5], part), 6)
    return {
        "basis": noise(part_splits[0], (NX, NY, NZ, R), R ** -0.5, 0.25, ((0, 4), (1, 4))),
        "kappa": jnp.clip(jnp.exp(math.log(1.0) - 2.3025851 * jax.random.uniform(part_splits[1], (NX, NY, NZ), jnp.float32) ** block_scale(part_splits[1], (NX, NY, NZ), ((0, 4), (1, 4)), -0.2, 0.2)), 0.1, 1.0),
        "velocity": jnp.clip(jax.random.uniform(part_splits[2], (3, P_SIZE), jnp.float32, -2.0, 2.0), -2.0, 2.0),
        "coefficients": noise(part_splits[3], (P_SIZE, R), 1.0, 6.0, (), jnp.float32),
        "propagator": noise(part_splits[4], (R, R), R ** -0.5, 0.25, (), jnp.float32),
    }


step_size = 4.0

def forcing_of(padded, kappa, velocity):
    center = padded[1:-1, 1:-1, 1:-1].astype(jnp.float32)
    x_next = padded[2:, 1:-1, 1:-1].astype(jnp.float32)
    x_prev = padded[:-2, 1:-1, 1:-1].astype(jnp.float32)
    y_next = padded[1:-1, 2:, 1:-1].astype(jnp.float32)
    y_prev = padded[1:-1, :-2, 1:-1].astype(jnp.float32)
    z_next = padded[1:-1, 1:-1, 2:].astype(jnp.float32)
    z_prev = padded[1:-1, 1:-1, :-2].astype(jnp.float32)
    spread = x_next + x_prev + y_next + y_prev + z_next + z_prev - 6.0 * center
    carried = velocity[0] * (x_next * x_next - x_prev * x_prev)
    carried = carried + velocity[1] * (y_next * y_next - y_prev * y_prev)
    carried = carried + velocity[2] * (z_next * z_next - z_prev * z_prev)
    result = kappa[..., None] * spread - 0.25 * carried
    return result.astype(jnp.bfloat16)

def reference(basis, kappa, velocity, coefficients, propagator):
    scale = 1.0 / jnp.sqrt(jnp.float32(NX * NY * NZ))
    state = coefficients
    block_ids = jnp.arange(N_WIDE).astype(jnp.int32)
    for step in range(ITERS):
        lift_rows = state.astype(jnp.bfloat16)

        def lift_block(index):
            rows = lax.dynamic_slice_in_dim(basis, index * CX, CX, 0).reshape(CX * NY * NZ, R)
            made = lax.dot_general(rows, lift_rows, (((1,), (1,)), ((), ())), preferred_element_type=jnp.float32)
            return made.astype(jnp.bfloat16)
        lifted = lax.map(lift_block, block_ids).reshape(NX, NY, NZ, P_SIZE)
        padded = jnp.pad(lifted, ((1, 1), (1, 1), (1, 1), (0, 0)))

        def project_block(total, index):
            window = lax.dynamic_slice_in_dim(padded, index * CX, CX + 2, 0)
            local_kappa = lax.dynamic_slice_in_dim(kappa, index * CX, CX, 0)
            forcing = forcing_of(window, local_kappa, velocity).reshape(CX * NY * NZ, P_SIZE)
            rows = lax.dynamic_slice_in_dim(basis, index * CX, CX, 0).reshape(CX * NY * NZ, R)
            term = lax.dot_general(forcing, rows, (((0,), (0,)), ((), ())), preferred_element_type=jnp.float32)
            return (total + term, None)
        total, unused = lax.scan(project_block, jnp.zeros((P_SIZE, R), jnp.float32), block_ids)
        projected = total * scale
        update = state + step_size * projected
        state = update + jnp.dot(update, propagator.T, precision=lax.Precision.HIGHEST, preferred_element_type=jnp.float32)
    return state
```

```python
import functools
import math

import jax
import jax.numpy as jnp
from jax import lax
from jax.experimental import pallas as pl
from jax.experimental.pallas import tpu as pltpu
from jax.sharding import PartitionSpec as P

ITERS = 2
WIRE = jnp.float32
PAD = 8

step_size = 4.0

NT = (((1,), (1,)), ((), ()))
NN = (((1,), (0,)), ((), ()))


def peer(me, offset):
    result, bit = me, 1
    while bit <= offset:
        if offset & bit:
            result = result + (1 - 2 * ((me // bit) % 2)) * bit
        bit *= 2
    return result


def dot(a, b, dims):
    return lax.dot_general(a, b, dims, preferred_element_type=jnp.float32)


def kernel(
    sizes, wide, narrow, scale,
    basis_ref, kappa_ref, velocity_ref, coefficients_ref, propagator_ref, out_ref,
    faces, halo_x, halo_y, field, forcing_ref, turned, g_high, g_low,
    partial, landed_w, reduced, landed_n, gathered,
    halo_send, halo_recv, w_send, w_recv, n_send, n_recv, an_send, an_recv, aw_send, aw_recv,
):
    size_x, size_y, size_z = sizes
    rows = size_y * size_z
    samples, modes = coefficients_ref.shape
    owned = samples // (wide * narrow)
    chunk = owned * narrow
    me_w, me_n = lax.axis_index("wide"), lax.axis_index("narrow")

    halo_x[...] = jnp.zeros_like(halo_x)
    halo_y[...] = jnp.zeros_like(halo_y)
    barrier = pltpu.get_barrier_semaphore()
    for e in range(1, wide):
        pl.semaphore_signal(barrier, inc=1, device_id={"wide": peer(me_w, e)}, device_id_type=pl.DeviceIdType.MESH)
    for d in range(1, narrow):
        pl.semaphore_signal(barrier, inc=1, device_id={"narrow": peer(me_n, d)}, device_id_type=pl.DeviceIdType.MESH)

    for x in range(size_x):
        at = x * rows
        faces[0, x * size_z:(x + 1) * size_z, :] = basis_ref[at:at + size_z, :]
        faces[1, x * size_z:(x + 1) * size_z, :] = basis_ref[at + rows - size_z:at + rows, :]
    g_high[...] = propagator_ref[...].astype(jnp.bfloat16)
    g_low[...] = (propagator_ref[...] - g_high[...].astype(jnp.float32)).astype(jnp.bfloat16)

    pl.semaphore_wait(barrier, wide + narrow - 2)

    def remote(src, dst, send, recv, **where):
        return pltpu.make_async_remote_copy(
            src_ref=src, dst_ref=dst, send_sem=send, recv_sem=recv,
            device_id=where, device_id_type=pl.DeviceIdType.MESH,
        )

    last = (size_x - 1) * rows
    halos = (
        (remote(faces.at[1], halo_y.at[0], halo_send.at[0], halo_recv.at[0], narrow=lax.rem(me_n + 1, narrow)),
         me_n < narrow - 1, me_n > 0),
        (remote(faces.at[0], halo_y.at[1], halo_send.at[1], halo_recv.at[1], narrow=lax.rem(me_n + narrow - 1, narrow)),
         me_n > 0, me_n < narrow - 1),
        (remote(basis_ref.at[pl.ds(last, rows)], halo_x.at[0], halo_send.at[2], halo_recv.at[2], wide=lax.rem(me_w + 1, wide)),
         me_w < wide - 1, me_w > 0),
        (remote(basis_ref.at[pl.ds(0, rows)], halo_x.at[1], halo_send.at[3], halo_recv.at[3], wide=lax.rem(me_w + wide - 1, wide)),
         me_w > 0, me_w < wide - 1),
    )
    for copy, sends, receives in halos:
        pl.when(sends)(copy.start)

    z_index = lax.broadcasted_iota(jnp.int32, (rows, samples), 0) % size_z
    first_row = (me_w * narrow + me_n) * owned
    if owned % 8 == 0:
        first_row = pl.multiple_of(first_row, 8)
    state = coefficients_ref[pl.ds(first_row, owned), :]
    lift_rows = coefficients_ref[...].astype(jnp.bfloat16)
    pending = []

    def lifted(of):
        return dot(of, lift_rows, NT).astype(jnp.bfloat16).astype(jnp.float32)

    for step in range(ITERS):
        field[1:size_x + 1, PAD:PAD + rows, :] = lifted(basis_ref[...]).reshape(size_x, rows, samples)
        if step == 0:
            for copy, sends, receives in halos:
                pl.when(receives)(copy.wait_recv)
        field[0, PAD:PAD + rows, :] = lifted(halo_x[0])
        field[size_x + 1, PAD:PAD + rows, :] = lifted(halo_x[1])
        before, after = lifted(halo_y[0]), lifted(halo_y[1])
        for x in range(size_x):
            field[x + 1, PAD - size_z:PAD, :] = before[x * size_z:(x + 1) * size_z]
            field[x + 1, PAD + rows:PAD + rows + size_z, :] = after[x * size_z:(x + 1) * size_z]

        def slab(x, carry):
            center = field[x + 1, PAD:PAD + rows, :]
            x_next = field[x + 2, PAD:PAD + rows, :]
            x_prev = field[x, PAD:PAD + rows, :]
            y_next = field[x + 1, PAD + size_z:PAD + rows + size_z, :]
            y_prev = field[x + 1, PAD - size_z:PAD + rows - size_z, :]
            z_next = jnp.where(z_index < size_z - 1, field[x + 1, PAD + 1:PAD + rows + 1, :], 0.0)
            z_prev = jnp.where(z_index > 0, field[x + 1, PAD - 1:PAD + rows - 1, :], 0.0)
            spread = x_next + x_prev + y_next + y_prev + z_next + z_prev - 6.0 * center
            carried = velocity_ref[0:1, :] * (x_next * x_next - x_prev * x_prev)
            carried = carried + velocity_ref[1:2, :] * (y_next * y_next - y_prev * y_prev)
            carried = carried + velocity_ref[2:3, :] * (z_next * z_next - z_prev * z_prev)
            at = pl.multiple_of(x * rows, rows)
            result = kappa_ref[pl.ds(at, rows), :] * spread - 0.25 * carried
            forcing_ref[pl.ds(at, rows), :] = result.astype(jnp.bfloat16)
            return carry

        lax.fori_loop(0, size_x, slab, 0, unroll=4)
        turned[...] = forcing_ref[...].T

        def projected(target):
            at = pl.multiple_of(target * chunk, chunk)
            return dot(turned[pl.ds(at, chunk), :], basis_ref[...], NN)

        copies = []
        for e in reversed(range(1, wide)):
            target = peer(me_w, e)
            partial[step, e - 1] = projected(target).astype(WIRE)
            copy = remote(partial.at[step, e - 1], landed_w.at[step, e - 1], w_send.at[step, e - 1], w_recv.at[step, e - 1], wide=target)
            copy.start()
            copies.append((e, copy))
        total = projected(me_w)
        for e, copy in reversed(copies):
            copy.wait_recv()
            total = total + landed_w[step, e - 1].astype(jnp.float32)
            pending.append(copy)
        for n in range(narrow):
            reduced[step, n] = total[n * owned:(n + 1) * owned].astype(WIRE)
        copies = []
        for d in reversed(range(1, narrow)):
            target = peer(me_n, d)
            copy = remote(reduced.at[step, target], landed_n.at[step, d - 1], n_send.at[step, d - 1], n_recv.at[step, d - 1], narrow=target)
            copy.start()
            copies.append((d, copy))
        summed = reduced[step, me_n].astype(jnp.float32)
        for d, copy in reversed(copies):
            copy.wait_recv()
            summed = summed + landed_n[step, d - 1].astype(jnp.float32)
            pending.append(copy)

        update = state + step_size * (summed * scale)
        high = update.astype(jnp.bfloat16)
        low = (update - high.astype(jnp.float32)).astype(jnp.bfloat16)
        small = dot(high, g_low[...], NT) + dot(low, g_high[...], NT)
        state = update + (dot(high, g_high[...], NT) + small)

        if step + 1 < ITERS:
            gathered[step, me_w, me_n] = state.astype(jnp.bfloat16)
            along = []
            for d in reversed(range(1, narrow)):
                block = gathered.at[step, me_w, me_n]
                copy = remote(block, block, an_send.at[step, d - 1], an_recv.at[step, d - 1], narrow=peer(me_n, d))
                copy.start()
                along.append((d, copy))
            across = []

            def forward(d):
                block = gathered.at[step, me_w, peer(me_n, d)]
                for e in reversed(range(1, wide)):
                    copy = remote(block, block, aw_send.at[step, e - 1, d], aw_recv.at[step, e - 1, d], wide=peer(me_w, e))
                    copy.start()
                    across.append(copy)

            forward(0)
            for d, copy in reversed(along):
                copy.wait_recv()
                pending.append(copy)
                forward(d)
            for copy in across:
                copy.wait_recv()
                pending.append(copy)
            lift_rows = gathered[step].reshape(samples, modes)

    out_ref[...] = state
    for copy in pending:
        copy.wait_send()
    for copy, sends, receives in halos:
        pl.when(sends)(copy.wait_send)


def body(basis, kappa, velocity, coefficients, propagator):
    size_x, size_y, size_z, modes = basis.shape
    samples = coefficients.shape[0]
    wide, narrow = lax.axis_size("wide"), lax.axis_size("narrow")
    owned = samples // (wide * narrow)
    chunk = owned * narrow
    cells, rows = size_x * size_y * size_z, size_y * size_z
    scale = 1.0 / math.sqrt(cells * wide * narrow)
    f32, bf16 = jnp.float32, jnp.bfloat16
    dma = pltpu.SemaphoreType.DMA
    vmem = pl.BlockSpec(memory_space=pltpu.VMEM)
    return pl.pallas_call(
        functools.partial(kernel, (size_x, size_y, size_z), wide, narrow, scale),
        out_shape=jax.ShapeDtypeStruct((owned, modes), f32),
        in_specs=[vmem] * 5,
        out_specs=vmem,
        scratch_shapes=[
            pltpu.VMEM((2, size_x * size_z, modes), bf16),
            pltpu.VMEM((2, rows, modes), bf16),
            pltpu.VMEM((2, size_x * size_z, modes), bf16),
            pltpu.VMEM((size_x + 2, rows + 2 * PAD, samples), f32),
            pltpu.VMEM((cells, samples), bf16),
            pltpu.VMEM((samples, cells), bf16),
            pltpu.VMEM((modes, modes), bf16),
            pltpu.VMEM((modes, modes), bf16),
            pltpu.VMEM((ITERS, wide - 1, chunk, modes), WIRE),
            pltpu.VMEM((ITERS, wide - 1, chunk, modes), WIRE),
            pltpu.VMEM((ITERS, narrow, owned, modes), WIRE),
            pltpu.VMEM((ITERS, narrow - 1, owned, modes), WIRE),
            pltpu.VMEM((ITERS - 1, wide, narrow, owned, modes), bf16),
            dma((4,)), dma((4,)),
            dma((ITERS, wide - 1)), dma((ITERS, wide - 1)),
            dma((ITERS, narrow - 1)), dma((ITERS, narrow - 1)),
            dma((ITERS - 1, narrow - 1)), dma((ITERS - 1, narrow - 1)),
            dma((ITERS - 1, wide - 1, narrow)), dma((ITERS - 1, wide - 1, narrow)),
        ],
        compiler_params=pltpu.CompilerParams(
            collective_id=0, has_side_effects=True, vmem_limit_bytes=48 * 1024 * 1024
        ),
    )(basis.reshape(cells, modes), kappa.reshape(cells, 1), velocity, coefficients, propagator)


def solution(mesh):
    placed = (
        P(("groups", "wide"), "narrow", None, None),
        P(("groups", "wide"), "narrow", None),
        P(None, "groups"),
        P("groups", None),
        P("groups", None),
    )
    return jax.shard_map(
        body,
        mesh=mesh,
        in_specs=placed,
        out_specs=P(("groups", "wide", "narrow"), None),
        check_vma=False,
    )
```

```python
import functools
import math

import jax
import jax.numpy as jnp
from jax import lax
from jax.experimental import pallas as pl
from jax.experimental.pallas import tpu as pltpu
from jax.sharding import PartitionSpec as P

ITERS = 2
WIRE = jnp.bfloat16
PAD = 8

step_size = 4.0

NT = (((1,), (1,)), ((), ()))
NN = (((1,), (0,)), ((), ()))


def peer(me, offset):
    result, bit = me, 1
    while bit <= offset:
        if offset & bit:
            result = result + (1 - 2 * ((me // bit) % 2)) * bit
        bit *= 2
    return result


def dot(a, b, dims):
    return lax.dot_general(a, b, dims, preferred_element_type=jnp.float32)


def kernel(
    sizes, wide, narrow, scale,
    basis_ref, kappa_ref, velocity_ref, coefficients_ref, propagator_ref, out_ref,
    faces, halo_x, halo_y, field, forcing_ref, turned, g_high, g_low,
    pair_out, pair_in, reduced, kept, landed, gathered,
    halo_send, halo_recv, pair_send, pair_recv, r_send, r_recv, g_send, g_recv, f_send, f_recv,
):
    size_x, size_y, size_z = sizes
    rows = size_y * size_z
    samples, modes = coefficients_ref.shape
    owned = samples // (wide * narrow)
    chunk = owned * narrow
    me_w, me_n = lax.axis_index("wide"), lax.axis_index("narrow")

    halo_x[...] = jnp.zeros_like(halo_x)
    halo_y[...] = jnp.zeros_like(halo_y)
    barrier = pltpu.get_barrier_semaphore()
    greeted = [(e, 0) for e in range(1, wide)] + [(e, d) for e in range(0, wide, 2) for d in range(1, narrow)]
    for e, d in greeted:
        pl.semaphore_signal(
            barrier, inc=1, device_id={"wide": peer(me_w, e), "narrow": peer(me_n, d)},
            device_id_type=pl.DeviceIdType.MESH,
        )

    for x in range(size_x):
        at = x * rows
        faces[0, x * size_z:(x + 1) * size_z, :] = basis_ref[at:at + size_z, :]
        faces[1, x * size_z:(x + 1) * size_z, :] = basis_ref[at + rows - size_z:at + rows, :]
    g_high[...] = propagator_ref[...].astype(jnp.bfloat16)
    g_low[...] = (propagator_ref[...] - g_high[...].astype(jnp.float32)).astype(jnp.bfloat16)

    pl.semaphore_wait(barrier, len(greeted))

    def remote(src, dst, send, recv, **where):
        return pltpu.make_async_remote_copy(
            src_ref=src, dst_ref=dst, send_sem=send, recv_sem=recv,
            device_id=where, device_id_type=pl.DeviceIdType.MESH,
        )

    last = (size_x - 1) * rows
    halos = (
        (remote(faces.at[1], halo_y.at[0], halo_send.at[0], halo_recv.at[0], narrow=lax.rem(me_n + 1, narrow)),
         me_n < narrow - 1, me_n > 0),
        (remote(faces.at[0], halo_y.at[1], halo_send.at[1], halo_recv.at[1], narrow=lax.rem(me_n + narrow - 1, narrow)),
         me_n > 0, me_n < narrow - 1),
        (remote(basis_ref.at[pl.ds(last, rows)], halo_x.at[0], halo_send.at[2], halo_recv.at[2], wide=lax.rem(me_w + 1, wide)),
         me_w < wide - 1, me_w > 0),
        (remote(basis_ref.at[pl.ds(0, rows)], halo_x.at[1], halo_send.at[3], halo_recv.at[3], wide=lax.rem(me_w + wide - 1, wide)),
         me_w > 0, me_w < wide - 1),
    )
    for copy, sends, receives in halos:
        pl.when(sends)(copy.start)

    z_index = lax.broadcasted_iota(jnp.int32, (rows, samples), 0) % size_z
    first_row = (me_w * narrow + me_n) * owned
    if owned % 8 == 0:
        first_row = pl.multiple_of(first_row, 8)
    state = coefficients_ref[pl.ds(first_row, owned), :]
    lift_rows = coefficients_ref[...].astype(jnp.bfloat16)
    pending = []

    def lifted(of):
        return dot(of, lift_rows, NT).astype(jnp.bfloat16).astype(jnp.float32)

    for step in range(ITERS):
        field[1:size_x + 1, PAD:PAD + rows, :] = lifted(basis_ref[...]).reshape(size_x, rows, samples)
        if step == 0:
            for copy, sends, receives in halos:
                pl.when(receives)(copy.wait_recv)
        field[0, PAD:PAD + rows, :] = lifted(halo_x[0])
        field[size_x + 1, PAD:PAD + rows, :] = lifted(halo_x[1])
        before, after = lifted(halo_y[0]), lifted(halo_y[1])
        for x in range(size_x):
            field[x + 1, PAD - size_z:PAD, :] = before[x * size_z:(x + 1) * size_z]
            field[x + 1, PAD + rows:PAD + rows + size_z, :] = after[x * size_z:(x + 1) * size_z]

        def slab(x, carry):
            center = field[x + 1, PAD:PAD + rows, :]
            x_next = field[x + 2, PAD:PAD + rows, :]
            x_prev = field[x, PAD:PAD + rows, :]
            y_next = field[x + 1, PAD + size_z:PAD + rows + size_z, :]
            y_prev = field[x + 1, PAD - size_z:PAD + rows - size_z, :]
            z_next = jnp.where(z_index < size_z - 1, field[x + 1, PAD + 1:PAD + rows + 1, :], 0.0)
            z_prev = jnp.where(z_index > 0, field[x + 1, PAD - 1:PAD + rows - 1, :], 0.0)
            spread = x_next + x_prev + y_next + y_prev + z_next + z_prev - 6.0 * center
            carried = velocity_ref[0:1, :] * (x_next * x_next - x_prev * x_prev)
            carried = carried + velocity_ref[1:2, :] * (y_next * y_next - y_prev * y_prev)
            carried = carried + velocity_ref[2:3, :] * (z_next * z_next - z_prev * z_prev)
            at = pl.multiple_of(x * rows, rows)
            result = kappa_ref[pl.ds(at, rows), :] * spread - 0.25 * carried
            forcing_ref[pl.ds(at, rows), :] = result.astype(jnp.bfloat16)
            return carry

        lax.fori_loop(0, size_x, slab, 0, unroll=4)
        turned[...] = forcing_ref[...].T

        def projected(target):
            at = pl.multiple_of(target * chunk, chunk)
            return dot(turned[pl.ds(at, chunk), :], basis_ref[...], NN)

        pairs = []
        for i in reversed(range(wide // 2)):
            pair_out[step, i] = projected(peer(me_w, 2 * i + 1))
            copy = remote(
                pair_out.at[step, i], pair_in.at[step, i], pair_send.at[step, i], pair_recv.at[step, i],
                wide=peer(me_w, 1),
            )
            copy.start()
            pairs.append((i, copy))
        totals = [projected(peer(me_w, 2 * i)) for i, copy in pairs]
        spread_out = []
        for (i, copy), total in zip(pairs, totals):
            copy.wait_recv()
            pending.append(copy)
            total = total + pair_in[step, i]
            for n in range(narrow):
                block = total[n * owned:(n + 1) * owned]
                reduced[step, i, n] = block.astype(WIRE)
                if i == 0:
                    kept[n] = block
            for d in reversed(range(narrow)):
                if i == 0 and d == 0:
                    continue
                copy = remote(
                    reduced.at[step, i, peer(me_n, d)], landed.at[step, i, d],
                    r_send.at[step, i, d], r_recv.at[step, i, d],
                    wide=peer(me_w, 2 * i), narrow=peer(me_n, d),
                )
                copy.start()
                spread_out.append((i, d, copy))
        summed = kept[me_n]
        for i, d, copy in reversed(spread_out):
            copy.wait_recv()
            pending.append(copy)
            summed = summed + landed[step, i, d].astype(jnp.float32)

        update = state + step_size * (summed * scale)
        high = update.astype(jnp.bfloat16)
        low = (update - high.astype(jnp.float32)).astype(jnp.bfloat16)
        small = dot(high, g_low[...], NT) + dot(low, g_high[...], NT)
        state = update + (dot(high, g_high[...], NT) + small)

        if step + 1 < ITERS:
            gathered[step, me_w, me_n] = state.astype(jnp.bfloat16)
            others = [(i, d) for d in range(narrow) for i in range(wide // 2) if i + d > 0]
            direct, inside = {}, []
            own = gathered.at[step, me_w, me_n]
            for i, d in reversed(others):
                direct[i, d] = remote(
                    own, own, g_send.at[step, i, d], g_recv.at[step, i, d],
                    wide=peer(me_w, 2 * i), narrow=peer(me_n, d),
                )
                direct[i, d].start()

            def beside(i, d):
                block = gathered.at[step, peer(me_w, 2 * i), peer(me_n, d)]
                copy = remote(block, block, f_send.at[step, i, d], f_recv.at[step, i, d], wide=peer(me_w, 1))
                copy.start()
                inside.append(copy)

            beside(0, 0)
            for i, d in others:
                direct[i, d].wait_recv()
                pending.append(direct[i, d])
                beside(i, d)
            for copy in inside:
                copy.wait_recv()
                pending.append(copy)
            lift_rows = gathered[step].reshape(samples, modes)

    out_ref[...] = state
    for copy in pending:
        copy.wait_send()
    for copy, sends, receives in halos:
        pl.when(sends)(copy.wait_send)


def body(basis, kappa, velocity, coefficients, propagator):
    size_x, size_y, size_z, modes = basis.shape
    samples = coefficients.shape[0]
    wide, narrow = lax.axis_size("wide"), lax.axis_size("narrow")
    owned = samples // (wide * narrow)
    chunk = owned * narrow
    cells, rows = size_x * size_y * size_z, size_y * size_z
    scale = 1.0 / math.sqrt(cells * wide * narrow)
    f32, bf16 = jnp.float32, jnp.bfloat16
    dma = pltpu.SemaphoreType.DMA
    vmem = pl.BlockSpec(memory_space=pltpu.VMEM)
    return pl.pallas_call(
        functools.partial(kernel, (size_x, size_y, size_z), wide, narrow, scale),
        out_shape=jax.ShapeDtypeStruct((owned, modes), f32),
        in_specs=[vmem] * 5,
        out_specs=vmem,
        scratch_shapes=[
            pltpu.VMEM((2, size_x * size_z, modes), bf16),
            pltpu.VMEM((2, rows, modes), bf16),
            pltpu.VMEM((2, size_x * size_z, modes), bf16),
            pltpu.VMEM((size_x + 2, rows + 2 * PAD, samples), f32),
            pltpu.VMEM((cells, samples), bf16),
            pltpu.VMEM((samples, cells), bf16),
            pltpu.VMEM((modes, modes), bf16),
            pltpu.VMEM((modes, modes), bf16),
            pltpu.VMEM((ITERS, wide // 2, chunk, modes), f32),
            pltpu.VMEM((ITERS, wide // 2, chunk, modes), f32),
            pltpu.VMEM((ITERS, wide // 2, narrow, owned, modes), WIRE),
            pltpu.VMEM((narrow, owned, modes), f32),
            pltpu.VMEM((ITERS, wide // 2, narrow, owned, modes), WIRE),
            pltpu.VMEM((ITERS - 1, wide, narrow, owned, modes), bf16),
            dma((4,)), dma((4,)),
            dma((ITERS, wide // 2)), dma((ITERS, wide // 2)),
            dma((ITERS, wide // 2, narrow)), dma((ITERS, wide // 2, narrow)),
            dma((ITERS - 1, wide // 2, narrow)), dma((ITERS - 1, wide // 2, narrow)),
            dma((ITERS - 1, wide // 2, narrow)), dma((ITERS - 1, wide // 2, narrow)),
        ],
        compiler_params=pltpu.CompilerParams(
            collective_id=0, has_side_effects=True, vmem_limit_bytes=48 * 1024 * 1024
        ),
    )(basis.reshape(cells, modes), kappa.reshape(cells, 1), velocity, coefficients, propagator)


def solution(mesh):
    placed = (
        P(("groups", "wide"), "narrow", None, None),
        P(("groups", "wide"), "narrow", None),
        P(None, "groups"),
        P("groups", None),
        P("groups", None),
    )
    return jax.shard_map(
        body,
        mesh=mesh,
        in_specs=placed,
        out_specs=P(("groups", "wide", "narrow"), None),
        check_vma=False,
    )
```

```python
import functools
import math

import jax
import jax.numpy as jnp
from jax import lax
from jax.experimental import pallas as pl
from jax.experimental.pallas import tpu as pltpu
from jax.sharding import PartitionSpec as P

ITERS = 2
PAD = 8

step_size = 4.0

NT = (((1,), (1,)), ((), ()))
NN = (((1,), (0,)), ((), ()))


def peer(me, offset):
    result, bit = me, 1
    while bit <= offset:
        if offset & bit:
            result = result + (1 - 2 * ((me // bit) % 2)) * bit
        bit *= 2
    return result


def dot(a, b, dims):
    return lax.dot_general(a, b, dims, preferred_element_type=jnp.float32)


def kernel(
    sizes, wide, narrow, scale,
    basis_hbm, kappa_ref, velocity_ref, coefficients_hbm, propagator_hbm, out_ref,
    raw, coefficients_ref, propagator_ref, basis_ref, kappa_column, halo_x, halo_y, field, forcing_ref, turned, g_high, g_low,
    pair_out, pair_in, reduced, reduced_last, kept, landed, landed_last, gathered,
    load, halo_send, halo_recv, pair_send, pair_recv, r_send, r_recv, g_send, g_recv, f_send, f_recv,
):
    size_x, size_y, size_z = sizes
    rows = size_y * size_z
    samples, modes = coefficients_ref.shape
    cells, side = size_x * rows, size_x * size_z
    owned = samples // (wide * narrow)
    chunk = owned * narrow
    me_w, me_n = lax.axis_index("wide"), lax.axis_index("narrow")

    loads = [
        pltpu.make_async_copy(basis_hbm, raw, load.at[0]),
        pltpu.make_async_copy(coefficients_hbm, coefficients_ref, load.at[1]),
        pltpu.make_async_copy(propagator_hbm, propagator_ref, load.at[2]),
    ]
    for copy in loads:
        copy.start()
    halo_x[...] = jnp.zeros_like(halo_x)
    halo_y[...] = jnp.zeros_like(halo_y)
    barrier = pltpu.get_barrier_semaphore()
    greeted = [(e, 0) for e in range(1, wide)] + [(e, d) for e in range(0, wide, 2) for d in range(1, narrow)]
    for e, d in greeted:
        pl.semaphore_signal(
            barrier, inc=1, device_id={"wide": peer(me_w, e), "narrow": peer(me_n, d)},
            device_id_type=pl.DeviceIdType.MESH,
        )

    loads[0].wait()
    pl.semaphore_wait(barrier, len(greeted))

    def remote(src, dst, send, recv, **where):
        return pltpu.make_async_remote_copy(
            src_ref=src, dst_ref=dst, send_sem=send, recv_sem=recv,
            device_id=where, device_id_type=pl.DeviceIdType.MESH,
        )

    halos = (
        (remote(raw.at[size_x - 1], halo_x.at[0], halo_send.at[2], halo_recv.at[2], wide=lax.rem(me_w + 1, wide)),
         me_w < wide - 1, me_w > 0),
        (remote(raw.at[0], halo_x.at[1], halo_send.at[3], halo_recv.at[3], wide=lax.rem(me_w + wide - 1, wide)),
         me_w > 0, me_w < wide - 1),
        (remote(raw.at[:, size_y - 1], halo_y.at[0], halo_send.at[0], halo_recv.at[0], narrow=lax.rem(me_n + 1, narrow)),
         me_n < narrow - 1, me_n > 0),
        (remote(raw.at[:, 0], halo_y.at[1], halo_send.at[1], halo_recv.at[1], narrow=lax.rem(me_n + narrow - 1, narrow)),
         me_n > 0, me_n < narrow - 1),
    )
    for copy, sends, receives in halos:
        pl.when(sends)(copy.start)

    for x in range(size_x):
        basis_ref[x * rows:(x + 1) * rows, :] = raw[x].reshape(rows, modes)
    row = lax.broadcasted_iota(jnp.int32, (rows, size_y), 0)
    lane = lax.broadcasted_iota(jnp.int32, (rows, size_y), 1)
    for x in range(size_x):
        picked = jnp.zeros((rows, size_y), jnp.float32)
        for z in range(size_z):
            picked = jnp.where(row == lane * size_z + z, kappa_ref[x, z:z + 1, :], picked)
        kappa_column[x * rows:(x + 1) * rows, :] = jnp.sum(picked, axis=1, keepdims=True)
    loads[1].wait()

    z_index = lax.broadcasted_iota(jnp.int32, (rows, samples), 0) % size_z
    first_row = (me_w * narrow + me_n) * owned
    if owned % 8 == 0:
        first_row = pl.multiple_of(first_row, 8)
    state = coefficients_ref[pl.ds(first_row, owned), :]
    lift_rows = coefficients_ref[...].astype(jnp.bfloat16)
    pending = []

    def lifted(of):
        return dot(of, lift_rows, NT).astype(jnp.bfloat16).astype(jnp.float32)

    for step in range(ITERS):
        if step == 0:
            inner = lifted(basis_ref[0:cells, :])
            for copy, sends, receives in halos:
                pl.when(receives)(copy.wait_recv)
            for k in range(2):
                at = cells + k * rows
                basis_ref[at:at + rows, :] = halo_x[k].reshape(rows, modes)
                at = cells + 2 * rows + k * side
                basis_ref[at:at + side, :] = halo_y[k].reshape(side, modes)
            outer = lifted(basis_ref[cells:, :])
        else:
            both = lifted(basis_ref[...])
            inner, outer = both[:cells], both[cells:]
        field[1:size_x + 1, PAD:PAD + rows, :] = inner.reshape(size_x, rows, samples)
        field[0, PAD:PAD + rows, :] = outer[:rows]
        field[size_x + 1, PAD:PAD + rows, :] = outer[rows:2 * rows]
        before, after = outer[2 * rows:2 * rows + side], outer[2 * rows + side:]
        for x in range(size_x):
            field[x + 1, PAD - size_z:PAD, :] = before[x * size_z:(x + 1) * size_z]
            field[x + 1, PAD + rows:PAD + rows + size_z, :] = after[x * size_z:(x + 1) * size_z]

        def slab(x, carry):
            center = field[x + 1, PAD:PAD + rows, :]
            x_next = field[x + 2, PAD:PAD + rows, :]
            x_prev = field[x, PAD:PAD + rows, :]
            y_next = field[x + 1, PAD + size_z:PAD + rows + size_z, :]
            y_prev = field[x + 1, PAD - size_z:PAD + rows - size_z, :]
            z_next = jnp.where(z_index < size_z - 1, field[x + 1, PAD + 1:PAD + rows + 1, :], 0.0)
            z_prev = jnp.where(z_index > 0, field[x + 1, PAD - 1:PAD + rows - 1, :], 0.0)
            spread = x_next + x_prev + y_next + y_prev + z_next + z_prev - 6.0 * center
            carried = velocity_ref[0:1, :] * (x_next * x_next - x_prev * x_prev)
            carried = carried + velocity_ref[1:2, :] * (y_next * y_next - y_prev * y_prev)
            carried = carried + velocity_ref[2:3, :] * (z_next * z_next - z_prev * z_prev)
            at = pl.multiple_of(x * rows, rows)
            result = kappa_column[pl.ds(at, rows), :] * spread - 0.25 * carried
            forcing_ref[pl.ds(at, rows), :] = result.astype(jnp.bfloat16)
            return carry

        lax.fori_loop(0, size_x, slab, 0, unroll=4)
        turned[...] = forcing_ref[...].T

        def projected(target):
            at = pl.multiple_of(target * chunk, chunk)
            return dot(turned[pl.ds(at, chunk), :], basis_ref[0:cells, :], NN)

        final = step + 1 == ITERS
        ready = reduced_last if final else reduced.at[step]
        arrived = landed_last if final else landed.at[step]
        pairs = []
        for i in reversed(range(wide // 2)):
            pair_out[step, i] = projected(peer(me_w, 2 * i + 1))
            copy = remote(
                pair_out.at[step, i], pair_in.at[step, i], pair_send.at[step, i], pair_recv.at[step, i],
                wide=peer(me_w, 1),
            )
            copy.start()
            pairs.append((i, copy))
        totals = [projected(peer(me_w, 2 * i)) for i, copy in pairs]
        spread_out = []
        for (i, copy), total in zip(pairs, totals):
            copy.wait_recv()
            pending.append(copy)
            total = total + pair_in[step, i]
            for n in range(narrow):
                block = total[n * owned:(n + 1) * owned]
                ready[i, n] = block.astype(ready.dtype)
                if i == 0:
                    kept[n] = block
            for d in reversed(range(narrow)):
                if i == 0 and d == 0:
                    continue
                copy = remote(
                    ready.at[i, peer(me_n, d)], arrived.at[i, d],
                    r_send.at[step, i, d], r_recv.at[step, i, d],
                    wide=peer(me_w, 2 * i), narrow=peer(me_n, d),
                )
                copy.start()
                spread_out.append((i, d, copy))
        if step == 0:
            loads[2].wait()
            g_high[...] = propagator_ref[...].astype(jnp.bfloat16)
            g_low[...] = (propagator_ref[...] - g_high[...].astype(jnp.float32)).astype(jnp.bfloat16)
        summed = kept[me_n]
        for i, d, copy in reversed(spread_out):
            copy.wait_recv()
            pending.append(copy)
            summed = summed + arrived[i, d].astype(jnp.float32)

        update = state + step_size * (summed * scale)
        high = update.astype(jnp.bfloat16)
        low = (update - high.astype(jnp.float32)).astype(jnp.bfloat16)
        small = dot(high, g_low[...], NT) + dot(low, g_high[...], NT)
        state = update + (dot(high, g_high[...], NT) + small)

        if step + 1 < ITERS:
            gathered[step, me_w, me_n] = state.astype(jnp.bfloat16)
            others = [(i, d) for d in range(narrow) for i in range(wide // 2) if i + d > 0]
            direct, inside = {}, []
            own = gathered.at[step, me_w, me_n]
            for i, d in reversed(others):
                direct[i, d] = remote(
                    own, own, g_send.at[step, i, d], g_recv.at[step, i, d],
                    wide=peer(me_w, 2 * i), narrow=peer(me_n, d),
                )
                direct[i, d].start()

            def beside(i, d):
                block = gathered.at[step, peer(me_w, 2 * i), peer(me_n, d)]
                copy = remote(block, block, f_send.at[step, i, d], f_recv.at[step, i, d], wide=peer(me_w, 1))
                copy.start()
                inside.append(copy)

            beside(0, 0)
            for i, d in others:
                direct[i, d].wait_recv()
                pending.append(direct[i, d])
                beside(i, d)
            for copy in inside:
                copy.wait_recv()
                pending.append(copy)
            lift_rows = gathered[step].reshape(samples, modes)

    out_ref[...] = state
    for copy in pending:
        copy.wait_send()
    for copy, sends, receives in halos:
        pl.when(sends)(copy.wait_send)


def body(basis, kappa, velocity, coefficients, propagator):
    size_x, size_y, size_z, modes = basis.shape
    samples = coefficients.shape[0]
    wide, narrow = lax.axis_size("wide"), lax.axis_size("narrow")
    owned = samples // (wide * narrow)
    chunk = owned * narrow
    cells, rows = size_x * size_y * size_z, size_y * size_z
    scale = 1.0 / math.sqrt(cells * wide * narrow)
    f32, bf16 = jnp.float32, jnp.bfloat16
    dma = pltpu.SemaphoreType.DMA
    vmem = pl.BlockSpec(memory_space=pltpu.VMEM)
    hbm = pl.BlockSpec(memory_space=pltpu.HBM)
    return pl.pallas_call(
        functools.partial(kernel, (size_x, size_y, size_z), wide, narrow, scale),
        out_shape=jax.ShapeDtypeStruct((owned, modes), f32),
        in_specs=[hbm, vmem, vmem, hbm, hbm],
        out_specs=vmem,
        scratch_shapes=[
            pltpu.VMEM((size_x, size_y, size_z, modes), bf16),
            pltpu.VMEM((samples, modes), f32),
            pltpu.VMEM((modes, modes), f32),
            pltpu.VMEM((cells + 2 * (size_x + size_y) * size_z, modes), bf16),
            pltpu.VMEM((cells, 1), f32),
            pltpu.VMEM((2, size_y, size_z, modes), bf16),
            pltpu.VMEM((2, size_x, size_z, modes), bf16),
            pltpu.VMEM((size_x + 2, rows + 2 * PAD, samples), f32),
            pltpu.VMEM((cells, samples), bf16),
            pltpu.VMEM((samples, cells), bf16),
            pltpu.VMEM((modes, modes), bf16),
            pltpu.VMEM((modes, modes), bf16),
            pltpu.VMEM((ITERS, wide // 2, chunk, modes), f32),
            pltpu.VMEM((ITERS, wide // 2, chunk, modes), f32),
            pltpu.VMEM((ITERS - 1, wide // 2, narrow, owned, modes), f32),
            pltpu.VMEM((wide // 2, narrow, owned, modes), bf16),
            pltpu.VMEM((narrow, owned, modes), f32),
            pltpu.VMEM((ITERS - 1, wide // 2, narrow, owned, modes), f32),
            pltpu.VMEM((wide // 2, narrow, owned, modes), bf16),
            pltpu.VMEM((ITERS - 1, wide, narrow, owned, modes), bf16),
            dma((3,)), dma((4,)), dma((4,)),
            dma((ITERS, wide // 2)), dma((ITERS, wide // 2)),
            dma((ITERS, wide // 2, narrow)), dma((ITERS, wide // 2, narrow)),
            dma((ITERS - 1, wide // 2, narrow)), dma((ITERS - 1, wide // 2, narrow)),
            dma((ITERS - 1, wide // 2, narrow)), dma((ITERS - 1, wide // 2, narrow)),
        ],
        compiler_params=pltpu.CompilerParams(
            collective_id=0, has_side_effects=True, vmem_limit_bytes=60 * 1024 * 1024
        ),
    )(basis, kappa.transpose(0, 2, 1), velocity, coefficients, propagator)


def solution(mesh):
    placed = (
        P(("groups", "wide"), "narrow", None, None),
        P(("groups", "wide"), "narrow", None),
        P(None, "groups"),
        P("groups", None),
        P("groups", None),
    )
    return jax.shard_map(
        body,
        mesh=mesh,
        in_specs=placed,
        out_specs=P(("groups", "wide", "narrow"), None),
        check_vma=False,
    )
```
